512 devices in a mesh: row: 32 (over x, y), col: 16 (over z, core).
Axes of the slice: x: 4, y: 8, z: 8, core: 2. Of those that a mesh axis runs over, the one named last changes fastest.
Arguments:
- kernel: float32 [1, 8192, 2, 4096], P(None, 'row', None, 'col'), may hold values from 0 to 1.5, as said below
Outputs:
- factored: float32 [1, 8192, 2, 4096], P(None, 'row', None, 'col')
The draws below stay inside these ranges and needn't reach their ends.
Inputs may be any that keep to these rules, and one draw needn't show every extreme that they name: kernel is symmetric and positive definite with all eigenvalues at least about 0.5 (up to float32 rounding of the draw); its entries lie between 0 and 1.5.
All inputs are finite; a program needn't handle non-finite values.
Results may differ from the reference program's by a relative error of at most 0.0003.
Values sent between devices are 32-bit elements; how exact they have to be, the bound alone decides.
A program may use at most 64 MiB of HBM per device.

```python
import jax
import jax.numpy as jnp
from jax import lax

NB = 256
KBR = 1
PANELS = 3
FEAT = 256
ORDER = 8192
KBC = 2


def draw_kernel(key, part):
    points = jax.random.normal(key, (ORDER, FEAT), jnp.float32) / jnp.sqrt(jnp.float32(FEAT))
    squares = jnp.sum(points * points, axis=1)
    inner = jnp.dot(points, points.T, precision=lax.Precision.HIGHEST)
    dist = jnp.maximum(squares[:, None] + squares[None, :] - 2.0 * inner, 0.0)
    gauss = jnp.exp(-dist)
    gauss = 0.5 * (gauss + gauss.T)
    index = jnp.arange(ORDER, dtype=jnp.int32)
    matrix = jnp.where(index[:, None] == index[None, :], jnp.float32(1.5), gauss)
    return matrix.reshape(KBR, ORDER // KBR, KBC, ORDER // KBC)


def setup_inputs(seed: int = 0) -> dict:
    key_list = jax.random.split(jax.random.key(seed), 2)
    kernel = draw_kernel(jax.random.fold_in(key_list[1], 71), 0)
    return dict(kernel=kernel)


def reference(kernel):
    full = kernel.reshape(ORDER, ORDER)
    for step in range(PANELS):
        start = step * NB
        end = start + NB
        factor = jnp.linalg.cholesky(full[start:end, start:end])
        lower = lax.linalg.triangular_solve(factor, full[end:, start:end], left_side=False, lower=True, transpose_a=True)
        full = full.at[end:, end:].add(-jnp.dot(lower, lower.T, precision=lax.Precision.HIGHEST))
        full = full.at[start:end, start:end].set(factor)
        full = full.at[end:, start:end].set(lower)
        full = full.at[:start, start:end].set(jnp.float32(0.0))
    width = PANELS * NB
    full = full.at[:width, width:].set(jnp.float32(0.0))
    return full.reshape(KBR, ORDER // KBR, KBC, ORDER // KBC)
```

```python
import functools

import jax
import jax.numpy as jnp
from jax import lax
from jax.experimental import pallas as pl
from jax.experimental.pallas import tpu as pltpu
from jax.sharding import PartitionSpec as P

F32 = jnp.float32
BF16 = jnp.bfloat16
NB = 256
TB = 128
STEPS = 6
NX, NY, NQ = 4, 8, 16
VMEM = pltpu.VMEM
MESH = pl.DeviceIdType.MESH


def exchange(x_ref, b_ref, r_ref, d_ref, s1s, s1r, s2s, s2r, s3s, s3r,
             t1s, t1r, t2s, t2r, u1s, u1r, u2s, u2r, u3s, u3r, loc):
    p = lax.axis_index("row")
    q = lax.axis_index("col")
    x = p // NY
    y = p % NY

    barrier = pltpu.get_barrier_semaphore()

    def peer(dst, src, ssem, rsem, pp, qq):
        return pltpu.make_async_remote_copy(
            src_ref=src, dst_ref=dst, send_sem=ssem, recv_sem=rsem,
            device_id=(pp, qq), device_id_type=MESH)

    def row_of(xx, yy):
        return lax.rem(xx, NX) * NY + lax.rem(yy, NY)

    for k in range(1, NX):
        pl.semaphore_signal(barrier, inc=1, device_id=(row_of(x + k, y), q), device_id_type=MESH)
    for k in range(1, NY):
        pl.semaphore_signal(barrier, inc=1, device_id=(row_of(x, y + k), q), device_id_type=MESH)
    for k in range(1, NQ):
        pl.semaphore_signal(barrier, inc=1, device_id=(p, lax.rem(q + k, NQ)), device_id_type=MESH)
    pl.semaphore_wait(barrier, NX - 1 + NY - 1 + NQ - 1)

    xs = pl.ds(pl.multiple_of(x * 64, 64), 64)
    qs = pl.ds(pl.multiple_of(q * 16, 16), 16)

    for i in range(3):
        @pl.when((x == 0) & (y == i))
        def _():
            own = pltpu.make_async_copy(x_ref.at[:, 0:64, :], b_ref.at[i, :, 0:64, :], loc.at[0])
            own.start()
            for k in range(1, NX):
                ks = pl.ds(64 * k, 64)
                peer(b_ref.at[i, :, ks, :], x_ref.at[:, ks, :], s1s.at[k - 1], s1r,
                     row_of(x + k, y), q).start()
            own.wait()
    for j in range(3):
        @pl.when(q == j)
        def _():
            own = pltpu.make_async_copy(x_ref.at[0, qs, :], r_ref.at[j, qs, :], loc.at[1])
            own.start()
            for k in range(1, NQ):
                o = lax.rem(q + k, NQ)
                os = pl.ds(pl.multiple_of(o * 16, 16), 16)
                peer(r_ref.at[j, os, :], x_ref.at[0, os, :], t1s.at[k - 1], t1r.at[j], p, o).start()
            own.wait()
    for i in range(3):
        @pl.when(y == i)
        def _():
            @pl.when(x > 0)
            def _():
                peer(b_ref.at[i, :, xs, :], b_ref.at[i, :, xs, :], s1s.at[0], s1r, p, q).wait_recv()
            for k in range(1, NY):
                peer(b_ref.at[i, :, xs, :], b_ref.at[i, :, xs, :], s2s.at[k - 1], s2r.at[i],
                     row_of(x, y + k), q).start()
    for j in range(3):
        @pl.when(q != j)
        def _():
            peer(r_ref.at[j, qs, :], r_ref.at[j, qs, :], t1s.at[0], t1r.at[j], p, q).wait_recv()
    for k in range(1, NQ):
        peer(r_ref.at[:, qs, :], r_ref.at[:, qs, :], t2s.at[k - 1], t2r.at[k - 1],
             p, lax.rem(q + k, NQ)).start()
    for i in range(3):
        @pl.when(y != i)
        def _():
            peer(b_ref.at[i, :, xs, :], b_ref.at[i, :, xs, :], s2s.at[0], s2r.at[i], p, q).wait_recv()
    for k in range(1, NX):
        peer(b_ref.at[:, :, xs, :], b_ref.at[:, :, xs, :], s3s.at[k - 1], s3r.at[k - 1],
             row_of(x + k, y), q).start()
    for k in range(1, NQ):
        o = lax.rem(q + NQ - k, NQ)
        os = pl.ds(pl.multiple_of(o * 16, 16), 16)
        peer(r_ref.at[:, qs, :], r_ref.at[:, os, :], t2s.at[k - 1], t2r.at[k - 1], p, o).wait_recv()
    for i in range(3):
        n = 3 - i
        @pl.when((x == 0) & (y == i))
        def _():
            own = pltpu.make_async_copy(r_ref.at[i:3, 0:64, :], d_ref.at[i, i:3, 0:64, :], loc.at[0])
            own.start()
            for k in range(1, NX):
                ks = pl.ds(64 * k, 64)
                peer(d_ref.at[i, i:3, ks, :], r_ref.at[i:3, ks, :], u1s.at[k - 1], u1r,
                     row_of(x + k, y), q).start()
            own.wait()
    for i in range(3):
        @pl.when(y == i)
        def _():
            @pl.when(x > 0)
            def _():
                peer(d_ref.at[i, i:3, xs, :], d_ref.at[i, i:3, xs, :], u1s.at[0], u1r, p, q).wait_recv()
            for k in range(1, NY):
                peer(d_ref.at[i, i:3, xs, :], d_ref.at[i, i:3, xs, :], u2s.at[k - 1], u2r.at[i],
                     row_of(x, y + k), q).start()
    for i in range(3):
        @pl.when(y != i)
        def _():
            peer(d_ref.at[i, i:3, xs, :], d_ref.at[i, i:3, xs, :], u2s.at[0], u2r.at[i], p, q).wait_recv()
    for k in range(1, NX):
        for i in range(3):
            peer(d_ref.at[i, i:3, xs, :], d_ref.at[i, i:3, xs, :], u3s.at[k - 1, i], u3r.at[k - 1, i],
                 row_of(x + k, y), q).start()
    for k in range(1, NX):
        ox = lax.rem(x + NX - k, NX)
        os = pl.ds(pl.multiple_of(ox * 64, 64), 64)
        peer(b_ref.at[:, :, xs, :], b_ref.at[:, :, os, :], s3s.at[k - 1], s3r.at[k - 1], p, q).wait_recv()
        for i in range(3):
            peer(d_ref.at[i, i:3, xs, :], d_ref.at[i, i:3, os, :], u3s.at[k - 1, i], u3r.at[k - 1, i],
                 p, q).wait_recv()
    for i in range(3):
        @pl.when((x == 0) & (y == i))
        def _():
            for k in range(1, NX):
                ks = pl.ds(64 * k, 64)
                peer(b_ref.at[i, :, ks, :], x_ref.at[:, ks, :], s1s.at[k - 1], s1r, p, q).wait_send()
                peer(d_ref.at[i, i:3, ks, :], r_ref.at[i:3, ks, :], u1s.at[k - 1], u1r, p, q).wait_send()

        @pl.when(y == i)
        def _():
            for k in range(1, NY):
                peer(b_ref.at[i, :, xs, :], b_ref.at[i, :, xs, :], s2s.at[k - 1], s2r.at[i], p, q).wait_send()
                peer(d_ref.at[i, i:3, xs, :], d_ref.at[i, i:3, xs, :], u2s.at[k - 1], u2r.at[i], p, q).wait_send()

        @pl.when(q == i)
        def _():
            for k in range(1, NQ):
                peer(r_ref.at[i, qs, :], x_ref.at[0, qs, :], t1s.at[k - 1], t1r.at[i], p, q).wait_send()
    for k in range(1, NQ):
        peer(r_ref.at[:, qs, :], r_ref.at[:, qs, :], t2s.at[k - 1], t2r.at[k - 1], p, q).wait_send()
    for k in range(1, NX):
        peer(b_ref.at[:, :, xs, :], b_ref.at[:, :, xs, :], s3s.at[k - 1], s3r.at[k - 1], p, q).wait_send()
        for i in range(3):
            peer(d_ref.at[i, i:3, xs, :], d_ref.at[i, i:3, xs, :], u3s.at[k - 1, i], u3r.at[k - 1, i],
                 p, q).wait_send()


def gather(x):
    dma = pltpu.SemaphoreType.DMA
    return pl.pallas_call(
        exchange,
        out_shape=(jax.ShapeDtypeStruct((3, 2, NB, NB), F32),
                   jax.ShapeDtypeStruct((3, NB, NB), F32),
                   jax.ShapeDtypeStruct((3, 3, NB, NB), F32)),
        in_specs=[pl.BlockSpec(memory_space=VMEM)],
        out_specs=[pl.BlockSpec(memory_space=VMEM)] * 3,
        scratch_shapes=[
            dma((3,)), dma(()), dma((7,)), dma((3,)), dma((3,)), dma((3,)),
            dma((15,)), dma((3,)), dma((15,)), dma((15,)),
            dma((3,)), dma(()), dma((7,)), dma((3,)), dma((3, 3)), dma((3, 3)),
            dma((2,)),
        ],
        compiler_params=pltpu.CompilerParams(
            collective_id=0, has_side_effects=True, vmem_limit_bytes=48 << 20),
        name="exchange",
    )(x)


def factor_tile(M):
    n = len(M)
    sub = lax.broadcasted_iota(jnp.int32, (8, TB), 0)
    lane = lax.broadcasted_iota(jnp.int32, (8, TB), 1)
    M = list(M)
    E = [jnp.where(lane == sub + 8 * g, 1.0, 0.0).astype(F32) for g in range(n)]
    wide = lambda v: jnp.broadcast_to(v, (8, TB))
    out_u, out_e = [], []
    for g in range(n):
        V = [{h: wide(M[h][:, 8 * g + k:8 * g + k + 1]) for h in range(g, n)} for k in range(8)]
        d = V[0][g]
        for k in range(8):
            inv = 1.0 / wide(V[k][g][k:k + 1, :])
            for j in range(k + 1, 8):
                s = wide(V[k][g][j:j + 1, :])
                V[j][g] = V[j][g] - (V[k][g] * s) * inv
                f = s * inv
                for h in range(g + 1, n):
                    V[j][h] = V[j][h] - V[k][h] * f
            if k:
                d = jnp.where(sub == k, V[k][g], d)
            mult = jnp.where(sub > k, V[k][g] * inv, 0.0)
            row_m, row_e = wide(M[g][k:k + 1, :]), wide(E[g][k:k + 1, :])
            M[g] = M[g] - mult * row_m
            E[g] = E[g] - mult * row_e
            for h in range(g + 1, n):
                c = V[k][h] * inv
                M[h] = M[h] - c * row_m
                E[h] = E[h] - c * row_e
        r = lax.rsqrt(d)
        out_u.append(M[g] * r)
        out_e.append(E[g] * r)
    return out_u, out_e


def split(a):
    hi = a.astype(BF16)
    return hi, (a - hi.astype(F32)).astype(BF16)


def left(a, axis):
    hi, lo = split(a)
    return jnp.concatenate([hi, lo, hi], axis)


def right(a, axis):
    hi, lo = split(a)
    return jnp.concatenate([hi, hi, lo], axis)


def mm(a, b):
    return jnp.dot(a, b, preferred_element_type=F32)


def mmt(a, b):
    return lax.dot_general(a, b, (((1,), (1,)), ((), ())), preferred_element_type=F32)


def solve(pos_ref, b_in, r_in, d_in, c_ref, o_ref, a_ref, b_ref, r_ref, acc_ref, inv_ref):
    p = pos_ref[0]
    q = pos_ref[1]
    for t in range(STEPS):
        i, h = divmod(t, 2)
        lo, hi = t * TB, (t + 1) * TB
        rows = slice(h * TB, h * TB + TB)
        if t == 0:
            tile = lambda g: d_in[0, 0, 8 * g:8 * g + 8, 0:TB]
        else:
            tile = lambda g: a_ref[lo + 8 * g:lo + 8 * g + 8, lo:hi]
        U, E = factor_tile([tile(g) for g in range(16)])
        for g in range(16):
            inv_ref[8 * g:8 * g + 8, :] = E[g]
        inv = inv_ref[...]
        inv_l = left(inv, 1)
        if t == 0:
            bt = jnp.concatenate([b_in[0, 0, 0:TB, :], b_in[0, 1, 0:TB, :]], 1)
            rt = r_in[0, :, 0:TB]
        else:
            bt = b_ref[lo:hi, :]
            rt = r_ref[:, lo:hi]
        ub = right(mm(inv_l, right(bt, 0)), 0)
        lt = mmt(left(rt, 1), right(inv, 1))
        r_ref[:, lo:hi] = lt
        lt_l = left(lt, 1)
        cur = c_ref[...] if t == 0 else acc_ref[...]
        acc_ref[...] = cur - mm(lt_l, ub)
        if t + 1 < STEPS:
            if t == 0:
                at = jnp.concatenate(
                    [d_in[0, 0, 0:TB, TB:], d_in[0, 1, 0:TB, :], d_in[0, 2, 0:TB, :]], 1)
            else:
                at = a_ref[lo:hi, hi:]
            ua = mm(inv_l, right(at, 0))
            ua_r = right(ua, 0)
            uat = left(ua.T, 1)
            if t == 0:
                for u in range(1, STEPS):
                    ui, uh = divmod(u, 2)
                    us = slice(uh * TB, uh * TB + TB)
                    rest = [d_in[ui, j, us, :] for j in range(ui, 3)]
                    rest[0] = rest[0][:, uh * TB:]
                    w = (STEPS - u) * TB
                    upd = mm(uat[(u - 1) * TB:u * TB, :], ua_r[:, (STEPS - 1) * TB - w:])
                    a_ref[u * TB:u * TB + TB, u * TB:] = jnp.concatenate(rest, 1) - upd
                    b_ref[u * TB:u * TB + TB, :] = jnp.concatenate(
                        [b_in[ui, 0, us, :], b_in[ui, 1, us, :]], 1) - mm(uat[(u - 1) * TB:u * TB, :], ub)
                r_ref[:, hi:] = jnp.concatenate(
                    [r_in[0, :, TB:], r_in[1], r_in[2]], 1) - mm(lt_l, ua_r)
            else:
                a_ref[hi:, hi:] = a_ref[hi:, hi:] - mm(uat, ua_r)
                b_ref[hi:, :] = b_ref[hi:, :] - mm(uat, ub)
                r_ref[:, hi:] = r_ref[:, hi:] - mm(lt_l, ua_r)
    keep = p >= 3
    o_ref[1] = jnp.where(keep, acc_ref[:, NB:], 0.0)

    @pl.when(q >= 3)
    def _():
        o_ref[0] = jnp.where(keep, acc_ref[:, :NB], 0.0)

    row = lax.broadcasted_iota(jnp.int32, (NB, NB), 0) + p * NB
    col = lax.broadcasted_iota(jnp.int32, (NB, NB), 1)
    for j in range(3):
        @pl.when(q == j)
        def _():
            o_ref[0] = jnp.where(row >= col + j * NB, r_ref[:, j * NB:(j + 1) * NB], 0.0)


def factor(pos, b, r, d, c):
    vm = pl.BlockSpec(memory_space=VMEM)
    return pl.pallas_call(
        solve,
        out_shape=jax.ShapeDtypeStruct((2, NB, NB), F32),
        in_specs=[pl.BlockSpec(memory_space=pltpu.SMEM), vm, vm, vm, vm],
        out_specs=vm,
        scratch_shapes=[
            VMEM((3 * NB, 3 * NB), F32), VMEM((3 * NB, 2 * NB), F32), VMEM((NB, 3 * NB), F32),
            VMEM((NB, 2 * NB), F32), VMEM((TB, TB), F32),
        ],
        compiler_params=pltpu.CompilerParams(vmem_limit_bytes=48 << 20),
        name="factor",
    )(pos, b, r, d, c)


def shards(kernel):
    x = kernel[0].transpose(1, 0, 2)
    pos = jnp.stack([lax.axis_index("row"), lax.axis_index("col")]).astype(jnp.int32)
    b, r, d = gather(x)
    c = jnp.concatenate([x[0], x[1]], axis=1)
    out = factor(pos, b, r, d, c)
    return out.transpose(1, 0, 2)[None]


def solution(mesh):
    spec = P(None, "row", None, "col")
    return jax.shard_map(shards, mesh=mesh, in_specs=(spec,), out_specs=spec, check_vma=False)
```

```python
import functools

import jax
import jax.numpy as jnp
from jax import lax
from jax.experimental import pallas as pl
from jax.experimental.pallas import tpu as pltpu
from jax.sharding import PartitionSpec as P

F32 = jnp.float32
BF16 = jnp.bfloat16
NB = 256
TB = 128
STEPS = 6
NX, NY, NQ = 4, 8, 16
VMEM = pltpu.VMEM
MESH = pl.DeviceIdType.MESH


def exchange(x_ref, b_ref, r_ref, d_ref, s1s, s1r, s2s, s2r, s3s, s3r,
             t1s, t1r, t2s, t2r, u1s, u1r, u2s, u2r, u3s, u3r, loc):
    p = lax.axis_index("row")
    q = lax.axis_index("col")
    x = p // NY
    y = p % NY

    barrier = pltpu.get_barrier_semaphore()

    def peer(dst, src, ssem, rsem, pp, qq):
        return pltpu.make_async_remote_copy(
            src_ref=src, dst_ref=dst, send_sem=ssem, recv_sem=rsem,
            device_id=(pp, qq), device_id_type=MESH)

    def row_of(xx, yy):
        return lax.rem(xx, NX) * NY + lax.rem(yy, NY)

    for k in range(1, NX):
        pl.semaphore_signal(barrier, inc=1, device_id=(row_of(x + k, y), q), device_id_type=MESH)
    for k in range(1, NY):
        pl.semaphore_signal(barrier, inc=1, device_id=(row_of(x, y + k), q), device_id_type=MESH)
    for k in range(1, NQ):
        pl.semaphore_signal(barrier, inc=1, device_id=(p, lax.rem(q + k, NQ)), device_id_type=MESH)
    pl.semaphore_wait(barrier, NX - 1 + NY - 1 + NQ - 1)

    xs = pl.ds(pl.multiple_of(x * 64, 64), 64)
    qs = pl.ds(pl.multiple_of(q * 16, 16), 16)

    for i in range(3):
        @pl.when((x == 0) & (y == i))
        def _():
            own = pltpu.make_async_copy(x_ref.at[:, 0:64, :], b_ref.at[i, :, 0:64, :], loc.at[0])
            own.start()
            for k in range(1, NX):
                ks = pl.ds(64 * k, 64)
                peer(b_ref.at[i, :, ks, :], x_ref.at[:, ks, :], s1s.at[k - 1], s1r,
                     row_of(x + k, y), q).start()
            own.wait()
    for j in range(3):
        @pl.when(q == j)
        def _():
            own = pltpu.make_async_copy(x_ref.at[0, qs, :], r_ref.at[j, qs, :], loc.at[1])
            own.start()
            for k in range(1, NQ):
                o = lax.rem(q + k, NQ)
                os = pl.ds(pl.multiple_of(o * 16, 16), 16)
                peer(r_ref.at[j, os, :], x_ref.at[0, os, :], t1s.at[k - 1], t1r.at[j], p, o).start()
            own.wait()
    for i in range(3):
        @pl.when(y == i)
        def _():
            @pl.when(x > 0)
            def _():
                peer(b_ref.at[i, :, xs, :], b_ref.at[i, :, xs, :], s1s.at[0], s1r, p, q).wait_recv()
            for k in range(1, NY):
                peer(b_ref.at[i, :, xs, :], b_ref.at[i, :, xs, :], s2s.at[k - 1], s2r.at[i],
                     row_of(x, y + k), q).start()
    for j in range(3):
        @pl.when(q != j)
        def _():
            peer(r_ref.at[j, qs, :], r_ref.at[j, qs, :], t1s.at[0], t1r.at[j], p, q).wait_recv()
    for k in range(1, NQ):
        peer(r_ref.at[:, qs, :], r_ref.at[:, qs, :], t2s.at[k - 1], t2r.at[k - 1],
             p, lax.rem(q + k, NQ)).start()
    for i in range(3):
        @pl.when(y != i)
        def _():
            peer(b_ref.at[i, :, xs, :], b_ref.at[i, :, xs, :], s2s.at[0], s2r.at[i], p, q).wait_recv()
    for k in range(1, NX):
        peer(b_ref.at[:, :, xs, :], b_ref.at[:, :, xs, :], s3s.at[k - 1], s3r.at[k - 1],
             row_of(x + k, y), q).start()
    for k in range(1, NQ):
        o = lax.rem(q + NQ - k, NQ)
        os = pl.ds(pl.multiple_of(o * 16, 16), 16)
        peer(r_ref.at[:, qs, :], r_ref.at[:, os, :], t2s.at[k - 1], t2r.at[k - 1], p, o).wait_recv()
    for i in range(3):
        n = 3 - i
        @pl.when((x == 0) & (y == i))
        def _():
            own = pltpu.make_async_copy(r_ref.at[i:3, 0:64, :], d_ref.at[i, i:3, 0:64, :], loc.at[0])
            own.start()
            for k in range(1, NX):
                ks = pl.ds(64 * k, 64)
                peer(d_ref.at[i, i:3, ks, :], r_ref.at[i:3, ks, :], u1s.at[k - 1], u1r,
                     row_of(x + k, y), q).start()
            own.wait()
    for i in range(3):
        @pl.when(y == i)
        def _():
            @pl.when(x > 0)
            def _():
                peer(d_ref.at[i, i:3, xs, :], d_ref.at[i, i:3, xs, :], u1s.at[0], u1r, p, q).wait_recv()
            for k in range(1, NY):
                peer(d_ref.at[i, i:3, xs, :], d_ref.at[i, i:3, xs, :], u2s.at[k - 1], u2r.at[i],
                     row_of(x, y + k), q).start()
    for i in range(3):
        @pl.when(y != i)
        def _():
            peer(d_ref.at[i, i:3, xs, :], d_ref.at[i, i:3, xs, :], u2s.at[0], u2r.at[i], p, q).wait_recv()
    for k in range(1, NX):
        for i in range(3):
            peer(d_ref.at[i, i:3, xs, :], d_ref.at[i, i:3, xs, :], u3s.at[k - 1, i], u3r.at[k - 1, i],
                 row_of(x + k, y), q).start()
    for k in range(1, NX):
        ox = lax.rem(x + NX - k, NX)
        os = pl.ds(pl.multiple_of(ox * 64, 64), 64)
        peer(b_ref.at[:, :, xs, :], b_ref.at[:, :, os, :], s3s.at[k - 1], s3r.at[k - 1], p, q).wait_recv()
        for i in range(3):
            peer(d_ref.at[i, i:3, xs, :], d_ref.at[i, i:3, os, :], u3s.at[k - 1, i], u3r.at[k - 1, i],
                 p, q).wait_recv()
    for i in range(3):
        @pl.when((x == 0) & (y == i))
        def _():
            for k in range(1, NX):
                ks = pl.ds(64 * k, 64)
                peer(b_ref.at[i, :, ks, :], x_ref.at[:, ks, :], s1s.at[k - 1], s1r, p, q).wait_send()
                peer(d_ref.at[i, i:3, ks, :], r_ref.at[i:3, ks, :], u1s.at[k - 1], u1r, p, q).wait_send()

        @pl.when(y == i)
        def _():
            for k in range(1, NY):
                peer(b_ref.at[i, :, xs, :], b_ref.at[i, :, xs, :], s2s.at[k - 1], s2r.at[i], p, q).wait_send()
                peer(d_ref.at[i, i:3, xs, :], d_ref.at[i, i:3, xs, :], u2s.at[k - 1], u2r.at[i], p, q).wait_send()

        @pl.when(q == i)
        def _():
            for k in range(1, NQ):
                peer(r_ref.at[i, qs, :], x_ref.at[0, qs, :], t1s.at[k - 1], t1r.at[i], p, q).wait_send()
    for k in range(1, NQ):
        peer(r_ref.at[:, qs, :], r_ref.at[:, qs, :], t2s.at[k - 1], t2r.at[k - 1], p, q).wait_send()
    for k in range(1, NX):
        peer(b_ref.at[:, :, xs, :], b_ref.at[:, :, xs, :], s3s.at[k - 1], s3r.at[k - 1], p, q).wait_send()
        for i in range(3):
            peer(d_ref.at[i, i:3, xs, :], d_ref.at[i, i:3, xs, :], u3s.at[k - 1, i], u3r.at[k - 1, i],
                 p, q).wait_send()


def factor_tile(M):
    n = len(M)
    sub = lax.broadcasted_iota(jnp.int32, (8, TB), 0)
    lane = lax.broadcasted_iota(jnp.int32, (8, TB), 1)
    M = list(M)
    E = [jnp.where(lane == sub + 8 * g, 1.0, 0.0).astype(F32) for g in range(n)]
    wide = lambda v: jnp.broadcast_to(v, (8, TB))
    out_u, out_e = [], []
    for g in range(n):
        V = [{h: wide(M[h][:, 8 * g + k:8 * g + k + 1]) for h in range(g, n)} for k in range(8)]
        d = V[0][g]
        for k in range(8):
            inv = 1.0 / wide(V[k][g][k:k + 1, :])
            for j in range(k + 1, 8):
                s = wide(V[k][g][j:j + 1, :])
                V[j][g] = V[j][g] - (V[k][g] * s) * inv
                f = s * inv
                for h in range(g + 1, n):
                    V[j][h] = V[j][h] - V[k][h] * f
            if k:
                d = jnp.where(sub == k, V[k][g], d)
            mult = jnp.where(sub > k, V[k][g] * inv, 0.0)
            row_m, row_e = wide(M[g][k:k + 1, :]), wide(E[g][k:k + 1, :])
            M[g] = M[g] - mult * row_m
            E[g] = E[g] - mult * row_e
            for h in range(g + 1, n):
                c = V[k][h] * inv
                M[h] = M[h] - c * row_m
                E[h] = E[h] - c * row_e
        r = lax.rsqrt(d)
        out_u.append(M[g] * r)
        out_e.append(E[g] * r)
    return out_u, out_e


def split(a):
    hi = a.astype(BF16)
    return hi, (a - hi.astype(F32)).astype(BF16)


def left(a, axis):
    hi, lo = split(a)
    return jnp.concatenate([hi, lo, hi], axis)


def right(a, axis):
    hi, lo = split(a)
    return jnp.concatenate([hi, hi, lo], axis)


def mm(a, b):
    return jnp.dot(a, b, preferred_element_type=F32)


def mmt(a, b):
    return lax.dot_general(a, b, (((1,), (1,)), ((), ())), preferred_element_type=F32)


def solve(b_in, r_in, d_in, c_ref, o_ref, a_ref, b_ref, r_ref, acc_ref, inv_ref):
    p = lax.axis_index("row")
    q = lax.axis_index("col")
    for t in range(STEPS):
        i, h = divmod(t, 2)
        lo, hi = t * TB, (t + 1) * TB
        rows = slice(h * TB, h * TB + TB)
        if t == 0:
            tile = lambda g: d_in[0, 0, 8 * g:8 * g + 8, 0:TB]
        else:
            tile = lambda g: a_ref[lo + 8 * g:lo + 8 * g + 8, lo:hi]
        U, E = factor_tile([tile(g) for g in range(16)])
        for g in range(16):
            inv_ref[8 * g:8 * g + 8, :] = E[g]
        inv = inv_ref[...]
        inv_l = left(inv, 1)
        if t == 0:
            bt = jnp.concatenate([b_in[0, 0, 0:TB, :], b_in[0, 1, 0:TB, :]], 1)
            rt = r_in[0, :, 0:TB]
        else:
            bt = b_ref[lo:hi, :]
            rt = r_ref[:, lo:hi]
        ub = right(mm(inv_l, right(bt, 0)), 0)
        lt = mmt(left(rt, 1), right(inv, 1))
        r_ref[:, lo:hi] = lt
        lt_l = left(lt, 1)
        cur = jnp.concatenate([c_ref[0], c_ref[1]], 1) if t == 0 else acc_ref[...]
        acc_ref[...] = cur - mm(lt_l, ub)
        if t + 1 < STEPS:
            if t == 0:
                at = jnp.concatenate(
                    [d_in[0, 0, 0:TB, TB:], d_in[0, 1, 0:TB, :], d_in[0, 2, 0:TB, :]], 1)
            else:
                at = a_ref[lo:hi, hi:]
            ua = mm(inv_l, right(at, 0))
            ua_r = right(ua, 0)
            uat = left(ua.T, 1)
            if t == 0:
                for u in range(1, STEPS):
                    ui, uh = divmod(u, 2)
                    us = slice(uh * TB, uh * TB + TB)
                    rest = [d_in[ui, j, us, :] for j in range(ui, 3)]
                    rest[0] = rest[0][:, uh * TB:]
                    w = (STEPS - u) * TB
                    upd = mm(uat[(u - 1) * TB:u * TB, :], ua_r[:, (STEPS - 1) * TB - w:])
                    a_ref[u * TB:u * TB + TB, u * TB:] = jnp.concatenate(rest, 1) - upd
                    b_ref[u * TB:u * TB + TB, :] = jnp.concatenate(
                        [b_in[ui, 0, us, :], b_in[ui, 1, us, :]], 1) - mm(uat[(u - 1) * TB:u * TB, :], ub)
                r_ref[:, hi:] = jnp.concatenate(
                    [r_in[0, :, TB:], r_in[1], r_in[2]], 1) - mm(lt_l, ua_r)
            else:
                a_ref[hi:, hi:] = a_ref[hi:, hi:] - mm(uat, ua_r)
                b_ref[hi:, :] = b_ref[hi:, :] - mm(uat, ub)
                r_ref[:, hi:] = r_ref[:, hi:] - mm(lt_l, ua_r)
    keep = p >= 3
    o_ref[1] = jnp.where(keep, acc_ref[:, NB:], 0.0)

    @pl.when(q >= 3)
    def _():
        o_ref[0] = jnp.where(keep, acc_ref[:, :NB], 0.0)

    row = lax.broadcasted_iota(jnp.int32, (NB, NB), 0) + p * NB
    col = lax.broadcasted_iota(jnp.int32, (NB, NB), 1)
    for j in range(3):
        @pl.when(q == j)
        def _():
            o_ref[0] = jnp.where(row >= col + j * NB, r_ref[:, j * NB:(j + 1) * NB], 0.0)


def body(x_ref, o_ref, b_in, r_in, d_in, a_ref, b_ref, r_ref, acc_ref, inv_ref, *sems):
    exchange(x_ref, b_in, r_in, d_in, *sems)
    solve(b_in, r_in, d_in, x_ref, o_ref, a_ref, b_ref, r_ref, acc_ref, inv_ref)


def factor(x):
    dma = pltpu.SemaphoreType.DMA
    vm = pl.BlockSpec(memory_space=VMEM)
    return pl.pallas_call(
        body,
        out_shape=jax.ShapeDtypeStruct((2, NB, NB), F32),
        in_specs=[vm],
        out_specs=vm,
        scratch_shapes=[
            VMEM((3, 2, NB, NB), F32), VMEM((3, NB, NB), F32), VMEM((3, 3, NB, NB), F32),
            VMEM((3 * NB, 3 * NB), F32), VMEM((3 * NB, 2 * NB), F32), VMEM((NB, 3 * NB), F32),
            VMEM((NB, 2 * NB), F32), VMEM((TB, TB), F32),
            dma((3,)), dma(()), dma((7,)), dma((3,)), dma((3,)), dma((3,)),
            dma((15,)), dma((3,)), dma((15,)), dma((15,)),
            dma((3,)), dma(()), dma((7,)), dma((3,)), dma((3, 3)), dma((3, 3)),
            dma((2,)),
        ],
        compiler_params=pltpu.CompilerParams(
            collective_id=0, has_side_effects=True, vmem_limit_bytes=48 << 20),
        name="factor",
    )(x)


def shards(kernel):
    return factor(kernel[0].transpose(1, 0, 2)).transpose(1, 0, 2)[None]


def solution(mesh):
    spec = P(None, "row", None, "col")
    return jax.shard_map(shards, mesh=mesh, in_specs=(spec,), out_specs=spec, check_vma=False)
```

```python
import functools

import jax
import jax.numpy as jnp
from jax import lax
from jax.experimental import pallas as pl
from jax.experimental.pallas import tpu as pltpu
from jax.sharding import PartitionSpec as P

F32 = jnp.float32
BF16 = jnp.bfloat16
NB = 256
TB = 128
STEPS = 6
NX, NY, NZ = 4, 8, 8
TILES = (("L", 0), (0, 1), ("L", 1), (0, 2), (0, 3), (1, 2), (1, 3), ("L", 2), (2, 3),
         (0, 4), (0, 5), (1, 4), (1, 5), (2, 4), (2, 5), ("L", 3), (3, 4), (3, 5),
         ("L", 4), (4, 5), ("L", 5))
SLOT = {name: k for k, name in enumerate(TILES)}
GROUPS = ((0, 2), (2, 7), (7, 15), (15, 18), (18, 20), (20, 21))
NG = len(GROUPS)
SR = TB // 8
FAR = (4, 3, 5, 2, 6, 1, 7)
VMEM = pltpu.VMEM
MESH = pl.DeviceIdType.MESH


def remote(src, dst, ssem, rsem, dev):
    return pltpu.make_async_remote_copy(
        src_ref=src, dst_ref=dst, send_sem=ssem, recv_sem=rsem,
        device_id=dev, device_id_type=MESH)


def factor_tile(M, done):
    n = len(M)
    sub = lax.broadcasted_iota(jnp.int32, (8, TB), 0)
    lane = lax.broadcasted_iota(jnp.int32, (8, TB), 1)
    M = list(M)
    E = [jnp.where(lane == sub + 8 * g, 1.0, 0.0).astype(F32) for g in range(n)]
    wide = lambda v: jnp.broadcast_to(v, (8, TB))
    for g in range(n):
        V = [{h: wide(M[h][:, 8 * g + k:8 * g + k + 1]) for h in range(g, n)} for k in range(8)]
        d = V[0][g]
        for k in range(8):
            inv = 1.0 / wide(V[k][g][k:k + 1, :])
            for j in range(k + 1, 8):
                s = wide(V[k][g][j:j + 1, :])
                V[j][g] = V[j][g] - (V[k][g] * s) * inv
                f = s * inv
                for h in range(g + 1, n):
                    V[j][h] = V[j][h] - V[k][h] * f
            if k:
                d = jnp.where(sub == k, V[k][g], d)
            mult = jnp.where(sub > k, V[k][g] * inv, 0.0)
            row_m, row_e = wide(M[g][k:k + 1, :]), wide(E[g][k:k + 1, :])
            M[g] = M[g] - mult * row_m
            E[g] = E[g] - mult * row_e
            for h in range(g + 1, n):
                c = V[k][h] * inv
                M[h] = M[h] - c * row_m
                E[h] = E[h] - c * row_e
        r = lax.rsqrt(d)
        done(g, M[g] * r, E[g] * r)


def split(a):
    hi = a.astype(BF16)
    return hi, (a - hi.astype(F32)).astype(BF16)


def left(a, axis):
    hi, lo = split(a)
    return jnp.concatenate([hi, lo, hi], axis)


def right(a, axis):
    hi, lo = split(a)
    return jnp.concatenate([hi, hi, lo], axis)


def mm(a, b):
    return jnp.dot(a, b, preferred_element_type=F32)


def mmt(a, b):
    return lax.dot_general(a, b, (((1,), (1,)), ((), ())), preferred_element_type=F32)


def body(x_ref, o_ref, b_ref, s_ref, r_ref, d_ref, t_ref, acc_ref, u_ref,
         b1s, b1r, b2s, b2r, b3s, b3r, b4s, b4r, r1s, r1r, r2s, r2r, r3s, r3r, ds, dr,
         zs, zr, ps, pr, gs, gr, ms, mr, loc):
    p = lax.axis_index("row")
    q = lax.axis_index("col")
    x = p // NY
    y = p % NY
    z = q // 2
    c = q % 2
    mate = (p, q + 1 - 2 * c)
    first = (p == 0) & (q == 0)
    late = (p > 0) | (q > 0)

    def on_x(k):
        return (lax.rem(x + k, NX) * NY + y, q)

    def on_y(k):
        return (x * NY + lax.rem(y + k, NY), q)

    def on_z(k):
        return (p, lax.rem(z + k, NZ) * 2 + c)

    barrier = pltpu.get_barrier_semaphore()

    def greet(dev):
        pl.semaphore_signal(barrier, inc=1, device_id=dev, device_id_type=MESH)

    for k in range(1, NX):
        greet(on_x(k))
    for k in range(1, NY):
        greet(on_y(k))
    for k in range(1, 2 * NZ):
        greet((p, lax.rem(q + k, 2 * NZ)))
    def part(g, o):
        lo, hi = GROUPS[g]
        return t_ref.at[lo:hi, pl.ds(pl.multiple_of(o * SR, SR), SR), :]

    def deal(g, o):
        return remote(part(g, o), part(g, o), zs.at[g, o], zr.at[g], (0, 2 * o + 1))

    def where(s, u):
        return (s // 2, u // 2, slice((s % 2) * 2, (s % 2) * 2 + 2), slice(None), slice(None),
                slice((u % 2) * TB, (u % 2) * TB + TB))

    def get(s, u):
        return d_ref[where(s, u)].reshape(TB, TB)

    def base(t):
        def done(g, u, e):
            t_ref[SLOT["L", t], 8 * g:8 * g + 8, :] = e
            if t < 2:
                u_ref[t, 8 * g:8 * g + 8, :] = u
            if t == 5 and g % 2:
                deal(NG - 1, g // 2).start()

        tile = get(t, t)
        factor_tile([tile[8 * g:8 * g + 8, :] for g in range(16)], done)

    def reach(t, cols):
        a = jnp.concatenate([get(t, u) for u in cols], 1) if len(cols) > 1 else get(t, cols[0])
        w = mm(left(t_ref[SLOT["L", t]], 1), right(a, 0))
        for k, u in enumerate(cols):
            t_ref[SLOT[t, u]] = w[:, k * TB:(k + 1) * TB]
        wr = right(w, 0)
        for s in range(t + 1, cols[-1] + 1):
            us = [u for u in cols if u >= s]
            k0 = (us[0] - cols[0]) * TB
            upd = mm(left(t_ref[SLOT[t, s]].T, 1), wr[:, k0:])
            for k, u in enumerate(us):
                d_ref[where(s, u)] = (get(s, u) - upd[:, k * TB:(k + 1) * TB]).reshape(2, 8, 8, TB)


    corner = ((1, 1), (1, 2), (2, 2))

    @pl.when(first)
    def _():
        for dev in corner:
            greet(dev)
        d_ref[0, 0] = x_ref[0]
        base(0)
        reach(0, (1,))
        base(1)
        pl.semaphore_wait(barrier, NX - 1 + NY - 1 + 2 * NZ - 1 + 3)

    near = functools.reduce(lambda a, b: a | b, [(p == i) & (q == j) for i, j in corner])
    plain = late & jnp.logical_not(near)

    @pl.when(near)
    def _():
        greet((0, 0))
        pl.semaphore_wait(barrier, NX - 1 + NY - 1 + 2 * NZ - 1 + 1)

    @pl.when(plain)
    def _():
        pl.semaphore_wait(barrier, NX - 1 + NY - 1 + 2 * NZ - 1)

    blocks = ((0, 1), (1, 1), (0, 2), (1, 2), (2, 2))
    dcopy = {}
    for k, (i, j) in enumerate(blocks):
        dcopy[i, j] = remote(x_ref.at[0], d_ref.at[i, j], ds, dr.at[k], (0, 0))

        @pl.when((p == i) & (q == j))
        def _():
            dcopy[i, j].start()

    def b1(i, k):
        o = lax.rem(x + k, NX)
        return remote(x_ref.at[:, o], s_ref, b1s.at[k - 1], b1r, on_x(k))

    def b1_in(i):
        return remote(s_ref, s_ref, b1s.at[0], b1r, (p, q))

    def b2(i, k, dealt=True):
        o = lax.rem(y + k, NY)
        src = s_ref.at[:, o] if dealt else x_ref.at[:, 0, o]
        return remote(src, b_ref.at[i, :, x, o], b2s.at[k - 1], b2r.at[i], on_y(k))

    def b2_in(i):
        return remote(b_ref.at[i, :, x, y], b_ref.at[i, :, x, y], b2s.at[0], b2r.at[i], (p, q))

    def b3(k, along_y):
        mine = b_ref.at[:, :, x, y]
        return remote(mine, mine, b3s.at[k - 1], b3r.at[k - 1], on_y(k) if along_y else on_x(k))

    def b3_in(k, along_y):
        theirs = b_ref.at[:, :, x, lax.rem(y + NY - k, NY)] if along_y else b_ref.at[:, :, lax.rem(x + NX - k, NX), y]
        return remote(theirs, theirs, b3s.at[k - 1], b3r.at[k - 1], (p, q))

    def b4(k):
        return remote(b_ref.at[:, :, x], b_ref.at[:, :, x], b4s.at[k - 1], b4r.at[k - 1], on_x(k))

    def b4_in(k):
        theirs = b_ref.at[:, :, lax.rem(x + NX - k, NX)]
        return remote(theirs, theirs, b4s.at[k - 1], b4r.at[k - 1], (p, q))

    def ring(h, up, far):
        o = lax.rem(y + (NY - far if up else far), NY)
        if h == 4:
            blk = b_ref.at[:, 0 if up else 1, :, o]
        else:
            blk = b_ref.at[:, :, :, o]
        k = 2 * (h - 1) + (0 if up else 1)
        return remote(blk, blk, b4s.at[k], b4r.at[k], on_y(1 if up else NY - 1))

    def hop(h):
        @pl.when(c == 1)
        def _():
            for up in (True, False):
                if h > 1:
                    ring(h - 1, up, h - 1).wait_recv()
            for up in (True, False):
                ring(h, up, h - 1).start()

    def mine16(o):
        return x_ref.at[0, o // 4, pl.ds(2 * lax.rem(o, 4), 2)]

    def r1(j, k):
        o = lax.rem(q + k, 2 * NZ)
        return remote(mine16(o), r_ref.at[j, o // 2, lax.rem(o, 2)], r1s.at[k - 1], r1r.at[j], (p, o))

    def r1_in(j):
        return remote(r_ref.at[j, z, c], r_ref.at[j, z, c], r1s.at[0], r1r.at[j], (p, q))

    def r2(k):
        return remote(r_ref.at[:, z, c], r_ref.at[:, z, c], r2s.at[k - 1], r2r.at[k - 1], on_z(k))

    def r2_in(k):
        o = lax.rem(z + NZ - k, NZ)
        return remote(r_ref.at[:, z, c], r_ref.at[:, o, c], r2s.at[k - 1], r2r.at[k - 1], (p, q))

    def r3():
        return remote(r_ref.at[:, :, c], r_ref.at[:, :, c], r3s, r3r, mate)

    def r3_in():
        return remote(r_ref.at[:, :, c], r_ref.at[:, :, 1 - c], r3s, r3r, mate)

    for i in range(3):
        @pl.when((x == 0) & (y == i))
        def _():
            own = pltpu.make_async_copy(x_ref.at[:, 0, i], b_ref.at[i, :, 0, i], loc.at[0])
            own.start()
            for k in (2, 1, 3):
                b1(i, k).start()
            for k in FAR:
                b2(i, k, False).start()
            own.wait()

        @pl.when(q == i)
        def _():
            own = pltpu.make_async_copy(mine16(q), r_ref.at[i, z, c], loc.at[1])
            own.start()
            for k in range(1, 2 * NZ):
                r1(i, k).start()
            own.wait()

    def send_b2():
        for i in range(3):
            @pl.when((x > 0) & (y == i))
            def _():
                b1_in(i).wait_recv()
                own = pltpu.make_async_copy(s_ref.at[:, i], b_ref.at[i, :, x, i], loc.at[0])
                own.start()
                for k in FAR:
                    b2(i, k).start()
                own.wait()

    def send_b3():
        for i in range(3):
            @pl.when(y != i)
            def _():
                b2_in(i).wait_recv()

        @pl.when(c == 0)
        def _():
            for k in FAR:
                b3(k, True).start()

        @pl.when(c == 1)
        def _():
            for k in (2, 1, 3):
                b3(k, False).start()

    def send_b4():
        @pl.when(c == 0)
        def _():
            for k in range(1, NY):
                b3_in(k, True).wait_recv()
            for k in (2, 1, 3):
                b4(k).start()

        @pl.when(c == 1)
        def _():
            for k in range(1, NX):
                b3_in(k, False).wait_recv()
        hop(1)

    def get_b4():
        @pl.when(c == 0)
        def _():
            for k in range(1, NX):
                b4_in(k).wait_recv()

        @pl.when(c == 1)
        def _():
            for up in (True, False):
                ring(4, up, 4).wait_recv()

    def drain():
        for i in range(3):
            @pl.when(y == i)
            def _():
                for k in range(1, NY):
                    b2(i, k).wait_send()

        @pl.when(c == 0)
        def _():
            for k in range(1, NY):
                b3(k, True).wait_send()
            for k in range(1, NX):
                b4(k).wait_send()

        @pl.when(c == 1)
        def _():
            for k in range(1, NX):
                b3(k, False).wait_send()
            for h in range(1, 5):
                for up in (True, False):
                    ring(h, up, h - 1).wait_send()
        for k in range(1, NZ):
            r2(k).wait_send()
        r3().wait_send()

    def send_r2():
        for j in range(3):
            @pl.when(q != j)
            def _():
                r1_in(j).wait_recv()
        for k in FAR:
            r2(k).start()

    def send_r3():
        for k in range(1, NZ):
            r2_in(k).wait_recv()
        r3().start()

    plane = tuple((k, functools.partial(on_y, f), (x == 0) & (y == 0)) for k, f in enumerate(FAR)) + tuple(
        (7 + k, functools.partial(on_x, f), x == 0) for k, f in enumerate((2, 1, 3)))

    def spread(g, arm, dev):
        return remote(part(g, z), part(g, z), ps.at[g, arm], zr.at[g], dev)

    def pick(g, k):
        return remote(part(g, z), part(g, z), gs.at[g, k - 1], gr.at[g, k - 1], on_z(k))

    def pick_in(g, k):
        o = lax.rem(z + NZ - k, NZ)
        return remote(part(g, o), part(g, o), gs.at[g, k - 1], gr.at[g, k - 1], (p, q))

    def share(g):
        lo, hi = GROUPS[g]
        return remote(t_ref.at[lo:hi], t_ref.at[lo:hi], ms.at[g], mr.at[g], mate)

    def pass_on(g):
        @pl.when(c == 1)
        def _():
            deal(g, 0).wait_recv()
            for arm, dev, cond in plane:
                @pl.when(cond)
                def _():
                    spread(g, arm, dev()).start()
            for k in FAR:
                pick(g, k).start()

    def take(g):
        @pl.when(c == 1)
        def _():
            for k in range(1, NZ):
                pick_in(g, k).wait_recv()

            @pl.when((p > 0) | (z > 0))
            def _():
                share(g).start()

        @pl.when(c == 0)
        def _():
            share(g).wait_recv()

    @pl.when(first)
    def _():
        def emit(g):
            for o in FAR + (0,):
                deal(g, o).start()

        emit(0)
        send_r2()
        dcopy[0, 1].wait_recv()
        dcopy[1, 1].wait_recv()
        reach(0, (2, 3))
        reach(1, (2, 3))
        emit(1)
        base(2)
        reach(2, (3,))
        send_b3()
        for j in range(3):
            dcopy[j, 2].wait_recv()
        reach(0, (4, 5))
        reach(1, (4, 5))
        reach(2, (4, 5))
        emit(2)
        base(3)
        reach(3, (4, 5))
        emit(3)
        send_b4()
        base(4)
        reach(4, (5,))
        emit(4)
        base(5)
        send_r3()
        low = lax.broadcasted_iota(jnp.int32, (TB, TB), 0) >= lax.broadcasted_iota(jnp.int32, (TB, TB), 1)
        o_ref[0, 0:TB, 0:TB] = jnp.where(low, u_ref[0].T, 0.0)
        o_ref[0, 0:TB, TB:] = jnp.zeros((TB, TB), F32)
        o_ref[0, TB:, 0:TB] = t_ref[SLOT[0, 1]].T
        o_ref[0, TB:, TB:] = jnp.where(low, u_ref[1].T, 0.0)
        o_ref[1] = jnp.zeros((NB, NB), F32)
        r3_in().wait_recv()
        get_b4()
        drain()
        for g in range(NG):
            for o in range(NZ):
                deal(g, o).wait_send()

    @pl.when(late)
    def _():
        def rcols(s):
            return (s // 2, slice(None), slice(None), slice(None), slice(None), slice((s % 2) * TB, (s % 2) * TB + TB))

        def brow(s):
            return [(s // 2, j, slice((s % 2) * 2, (s % 2) * 2 + 2)) for j in range(2)]

        def apply(t):
            inv = t_ref[SLOT["L", t]]
            bt = jnp.concatenate([b_ref[k].reshape(TB, NB) for k in brow(t)], 1)
            ub = right(mm(left(inv, 1), right(bt, 0)), 0)
            lt = mmt(left(r_ref[rcols(t)].reshape(NB, TB), 1), right(inv, 1))
            r_ref[rcols(t)] = lt.reshape(NZ, 2, 2, 8, TB)
            lt = left(lt, 1)
            cur = jnp.concatenate([x_ref[0].reshape(NB, NB), x_ref[1].reshape(NB, NB)], 1) if t == 0 else acc_ref[...]
            acc_ref[...] = cur - mm(lt, ub)
            for s in range(t + 1, STEPS):
                u = t_ref[SLOT[t, s]]
                upd = mm(left(u.T, 1), ub)
                for j, k in enumerate(brow(s)):
                    b_ref[k] = b_ref[k] - upd[:, j * NB:(j + 1) * NB].reshape(2, 8, 8, NB)
                r_ref[rcols(s)] = r_ref[rcols(s)] - mm(lt, right(u, 0)).reshape(NZ, 2, 2, 8, TB)

        send_b2()
        send_r2()
        send_b3()
        pass_on(0)
        send_r3()
        send_b4()
        pass_on(1)
        hop(2)
        take(0)
        pass_on(2)
        hop(3)
        take(1)
        r3_in().wait_recv()
        pass_on(3)
        hop(4)
        take(2)
        pass_on(4)
        take(3)
        pass_on(5)
        get_b4()
        drain()
        take(4)
        for t in range(5):
            apply(t)
        take(5)
        apply(5)
        keep = p >= 3
        o_ref[1] = jnp.where(keep, acc_ref[:, NB:], 0.0)

        @pl.when(q >= 3)
        def _():
            o_ref[0] = jnp.where(keep, acc_ref[:, :NB], 0.0)

        row = lax.broadcasted_iota(jnp.int32, (NB, NB), 0) + p * NB
        col = lax.broadcasted_iota(jnp.int32, (NB, NB), 1)
        for j in range(3):
            @pl.when(q == j)
            def _():
                o_ref[0] = jnp.where(row >= col + j * NB, r_ref[j].reshape(NB, NB), 0.0)

        for i, j in blocks:
            @pl.when((p == i) & (q == j))
            def _():
                dcopy[i, j].wait_send()

        @pl.when(c == 1)
        def _():
            for g in range(NG):
                for k in range(1, NZ):
                    pick(g, k).wait_send()
            for arm, dev, cond in plane:
                @pl.when(cond)
                def _():
                    for g in range(NG):
                        spread(g, arm, dev()).wait_send()

            @pl.when((p > 0) | (z > 0))
            def _():
                for g in range(NG):
                    share(g).wait_send()

    for i in range(3):
        @pl.when((x == 0) & (y == i))
        def _():
            for k in range(1, NX):
                b1(i, k).wait_send()

        @pl.when(q == i)
        def _():
            for k in range(1, 2 * NZ):
                r1(i, k).wait_send()


def factor(x):
    dma = pltpu.SemaphoreType.DMA
    vm = pl.BlockSpec(memory_space=VMEM)
    return pl.pallas_call(
        body,
        out_shape=jax.ShapeDtypeStruct((2, NB, NB), F32),
        in_specs=[vm],
        out_specs=vm,
        scratch_shapes=[
            VMEM((3, 2, NX, NY, 8, NB), F32), VMEM((2, NY, 8, NB), F32), VMEM((3, NZ, 2, 2, 8, NB), F32), VMEM((3, 3, NX, NY, 8, NB), F32),
            VMEM((len(TILES), TB, TB), F32), VMEM((NB, 2 * NB), F32), VMEM((2, TB, TB), F32),
            dma((3,)), dma(()), dma((7,)), dma((3,)), dma((7,)), dma((7,)), dma((8,)), dma((8,)),
            dma((15,)), dma((3,)), dma((7,)), dma((7,)), dma(()), dma(()), dma(()), dma((5,)),
            dma((NG, 8)), dma((NG,)), dma((NG, 10)), dma((NG,)), dma((NG, 7)), dma((NG, 7)), dma((NG,)), dma((NG,)),
            dma((2,)),
        ],
        compiler_params=pltpu.CompilerParams(
            collective_id=0, has_side_effects=True, vmem_limit_bytes=48 << 20),
        name="factor",
    )(x)


def shards(kernel):
    x = kernel[0].transpose(1, 0, 2).reshape(2, NX, NY, 8, NB)
    return factor(x).transpose(1, 0, 2)[None]


def solution(mesh):
    spec = P(None, "row", None, "col")
    return jax.shard_map(shards, mesh=mesh, in_specs=(spec,), out_specs=spec, check_vma=False)
```

```python
import functools

import jax
import jax.numpy as jnp
from jax import lax
from jax.experimental import pallas as pl
from jax.experimental.pallas import tpu as pltpu
from jax.sharding import PartitionSpec as P

F32 = jnp.float32
BF16 = jnp.bfloat16
NB = 256
TB = 128
STEPS = 6
NX, NY, NZ = 4, 8, 8
TILES = (("L", 0), (0, 1), ("L", 1), (0, 2), (0, 3), (1, 2), (1, 3), ("L", 2), (2, 3),
         (0, 4), (0, 5), (1, 4), (1, 5), (2, 4), (2, 5), ("L", 3), (3, 4), (3, 5),
         ("L", 4), (4, 5), ("L", 5))
SLOT = {name: k for k, name in enumerate(TILES)}
GROUPS = ((0, 2), (2, 7), (7, 15), (15, 18), (18, 20), (20, 21))
NG = len(GROUPS)
SR = TB // 8
FAR = (4, 3, 5, 2, 6, 1, 7)
VMEM = pltpu.VMEM
MESH = pl.DeviceIdType.MESH


def remote(src, dst, ssem, rsem, dev):
    return pltpu.make_async_remote_copy(
        src_ref=src, dst_ref=dst, send_sem=ssem, recv_sem=rsem,
        device_id=dev, device_id_type=MESH)


def factor_tile(M, done):
    n = len(M)
    sub = lax.broadcasted_iota(jnp.int32, (8, TB), 0)
    lane = lax.broadcasted_iota(jnp.int32, (8, TB), 1)
    M = list(M)
    E = [jnp.where(lane == sub + 8 * g, 1.0, 0.0).astype(F32) for g in range(n)]
    wide = lambda v: jnp.broadcast_to(v, (8, TB))
    for g in range(n):
        V = [{h: wide(M[h][:, 8 * g + k:8 * g + k + 1]) for h in range(g, n)} for k in range(8)]
        d = V[0][g]
        for k in range(8):
            inv = 1.0 / wide(V[k][g][k:k + 1, :])
            for j in range(k + 1, 8):
                s = wide(V[k][g][j:j + 1, :])
                V[j][g] = V[j][g] - (V[k][g] * s) * inv
                f = s * inv
                for h in range(g + 1, n):
                    V[j][h] = V[j][h] - V[k][h] * f
            if k:
                d = jnp.where(sub == k, V[k][g], d)
            mult = jnp.where(sub > k, V[k][g] * inv, 0.0)
            row_m, row_e = wide(M[g][k:k + 1, :]), wide(E[g][k:k + 1, :])
            M[g] = M[g] - mult * row_m
            E[g] = E[g] - mult * row_e
            for h in range(g + 1, n):
                c = V[k][h] * inv
                M[h] = M[h] - c * row_m
                E[h] = E[h] - c * row_e
        r = lax.rsqrt(d)
        done(g, M[g] * r, E[g] * r)


def split(a):
    hi = a.astype(BF16)
    return hi, (a - hi.astype(F32)).astype(BF16)


def left(a, axis):
    hi, lo = split(a)
    return jnp.concatenate([hi, lo, hi], axis)


def right(a, axis):
    hi, lo = split(a)
    return jnp.concatenate([hi, hi, lo], axis)


def mm(a, b):
    return jnp.dot(a, b, preferred_element_type=F32)


def mmt(a, b):
    return lax.dot_general(a, b, (((1,), (1,)), ((), ())), preferred_element_type=F32)


def body(x_ref, o_ref, b_ref, s_ref, r_ref, d_ref, t_ref, acc_ref, u_ref,
         b1s, b1r, b2s, b2r, b3s, b3r, b4s, b4r, r1s, r1r, r2s, r2r, r3s, r3r, ds, dr,
         zs, zr, ps, pr, gs, gr, ms, mr, loc):
    p = lax.axis_index("row")
    q = lax.axis_index("col")
    x = p // NY
    y = p % NY
    z = q // 2
    c = q % 2
    mate = (p, q + 1 - 2 * c)
    first = (p == 0) & (q == 0)
    late = (p > 0) | (q > 0)

    def on_x(k):
        return (lax.rem(x + k, NX) * NY + y, q)

    def on_y(k):
        return (x * NY + lax.rem(y + k, NY), q)

    def on_z(k):
        return (p, lax.rem(z + k, NZ) * 2 + c)

    barrier = pltpu.get_barrier_semaphore()

    def greet(dev):
        pl.semaphore_signal(barrier, inc=1, device_id=dev, device_id_type=MESH)

    for k in range(1, NX):
        greet(on_x(k))
    for k in range(1, NY):
        greet(on_y(k))
    for k in range(1, 2 * NZ):
        greet((p, lax.rem(q + k, 2 * NZ)))
    def part(g, o):
        lo, hi = GROUPS[g]
        return t_ref.at[lo:hi, pl.ds(pl.multiple_of(o * SR, SR), SR), :]

    def deal(g, o):
        return remote(part(g, o), part(g, o), zs.at[g, o], zr.at[g], (0, 2 * o + 1))

    def where(s, u):
        return (s // 2, u // 2, slice((s % 2) * 2, (s % 2) * 2 + 2), slice(None), slice(None),
                slice((u % 2) * TB, (u % 2) * TB + TB))

    def get(s, u):
        return d_ref[where(s, u)].reshape(TB, TB)

    def base(t):
        def done(g, u, e):
            t_ref[SLOT["L", t], 8 * g:8 * g + 8, :] = e
            if t < 2:
                u_ref[t, 8 * g:8 * g + 8, :] = u
            if t == 5 and g % 2:
                deal(NG - 1, g // 2).start()

        tile = get(t, t)
        factor_tile([tile[8 * g:8 * g + 8, :] for g in range(16)], done)

    def reach(t, cols):
        a = jnp.concatenate([get(t, u) for u in cols], 1) if len(cols) > 1 else get(t, cols[0])
        w = mm(left(t_ref[SLOT["L", t]], 1), right(a, 0))
        for k, u in enumerate(cols):
            t_ref[SLOT[t, u]] = w[:, k * TB:(k + 1) * TB]
        wr = right(w, 0)
        for s in range(t + 1, cols[-1] + 1):
            us = [u for u in cols if u >= s]
            k0 = (us[0] - cols[0]) * TB
            upd = mm(left(t_ref[SLOT[t, s]].T, 1), wr[:, k0:])
            for k, u in enumerate(us):
                d_ref[where(s, u)] = (get(s, u) - upd[:, k * TB:(k + 1) * TB]).reshape(2, 8, 8, TB)


    corner = ((1, 1), (1, 2), (2, 2))

    @pl.when(first)
    def _():
        for dev in corner:
            greet(dev)
        d_ref[0, 0] = x_ref[0]
        base(0)
        reach(0, (1,))
        base(1)
        pl.semaphore_wait(barrier, NX - 1 + NY - 1 + 2 * NZ - 1 + 3)

    near = functools.reduce(lambda a, b: a | b, [(p == i) & (q == j) for i, j in corner])
    plain = late & jnp.logical_not(near)

    @pl.when(near)
    def _():
        greet((0, 0))
        pl.semaphore_wait(barrier, NX - 1 + NY - 1 + 2 * NZ - 1 + 1)

    @pl.when(plain)
    def _():
        pl.semaphore_wait(barrier, NX - 1 + NY - 1 + 2 * NZ - 1)

    blocks = ((0, 1), (1, 1), (0, 2), (1, 2), (2, 2))
    dcopy = {}
    for k, (i, j) in enumerate(blocks):
        dcopy[i, j] = remote(x_ref.at[0], d_ref.at[i, j], ds, dr.at[k], (0, 0))

        @pl.when((p == i) & (q == j))
        def _():
            dcopy[i, j].start()

    def b1(i, k):
        o = lax.rem(x + k, NX)
        return remote(x_ref.at[:, o], s_ref, b1s.at[k - 1], b1r, on_x(k))

    def b1_in(i):
        return remote(s_ref, s_ref, b1s.at[0], b1r, (p, q))

    def b2(i, k, dealt=True):
        o = lax.rem(y + k, NY)
        src = s_ref.at[:, o] if dealt else x_ref.at[:, 0, o]
        return remote(src, b_ref.at[i, :, x, o], b2s.at[k - 1], b2r.at[i], on_y(k))

    def b2_in(i):
        return remote(b_ref.at[i, :, x, y], b_ref.at[i, :, x, y], b2s.at[0], b2r.at[i], (p, q))

    def b3(k, along_y):
        mine = b_ref.at[:, :, x, y]
        return remote(mine, mine, b3s.at[k - 1], b3r.at[k - 1], on_y(k) if along_y else on_x(k))

    def b3_in(k, along_y):
        theirs = b_ref.at[:, :, x, lax.rem(y + NY - k, NY)] if along_y else b_ref.at[:, :, lax.rem(x + NX - k, NX), y]
        return remote(theirs, theirs, b3s.at[k - 1], b3r.at[k - 1], (p, q))

    def b4(k):
        return remote(b_ref.at[:, :, x], b_ref.at[:, :, x], b4s.at[k - 1], b4r.at[k - 1], on_x(k))

    def b4_in(k):
        theirs = b_ref.at[:, :, lax.rem(x + NX - k, NX)]
        return remote(theirs, theirs, b4s.at[k - 1], b4r.at[k - 1], (p, q))

    def ring(h, up, far):
        o = lax.rem(y + (NY - far if up else far), NY)
        if h == 4:
            blk = b_ref.at[:, 0 if up else 1, :, o]
        else:
            blk = b_ref.at[:, :, :, o]
        k = 2 * (h - 1) + (0 if up else 1)
        return remote(blk, blk, b4s.at[k], b4r.at[k], on_y(1 if up else NY - 1))

    def hop(h):
        @pl.when(c == 1)
        def _():
            for up in (True, False):
                if h > 1:
                    ring(h - 1, up, h - 1).wait_recv()
            for up in (True, False):
                ring(h, up, h - 1).start()

    def mine16(o):
        return x_ref.at[0, o // 4, pl.ds(2 * lax.rem(o, 4), 2)]

    def r1(j, k):
        o = lax.rem(q + k, 2 * NZ)
        return remote(mine16(o), r_ref.at[j, o // 2, lax.rem(o, 2)], r1s.at[k - 1], r1r.at[j], (p, o))

    def r1_in(j):
        return remote(r_ref.at[j, z, c], r_ref.at[j, z, c], r1s.at[0], r1r.at[j], (p, q))

    def r2(k):
        return remote(r_ref.at[:, z, c], r_ref.at[:, z, c], r2s.at[k - 1], r2r.at[k - 1], on_z(k))

    def r2_in(k):
        o = lax.rem(z + NZ - k, NZ)
        return remote(r_ref.at[:, z, c], r_ref.at[:, o, c], r2s.at[k - 1], r2r.at[k - 1], (p, q))

    def r3():
        return remote(r_ref.at[:, :, c], r_ref.at[:, :, c], r3s, r3r, mate)

    def r3_in():
        return remote(r_ref.at[:, :, c], r_ref.at[:, :, 1 - c], r3s, r3r, mate)

    for i in range(3):
        @pl.when((x == 0) & (y == i))
        def _():
            own = pltpu.make_async_copy(x_ref.at[:, 0, i], b_ref.at[i, :, 0, i], loc.at[0])
            own.start()
            for k in (2, 1, 3):
                b1(i, k).start()
            for k in FAR:
                b2(i, k, False).start()
            own.wait()

        @pl.when((q == i) & (p > 0))
        def _():
            own = pltpu.make_async_copy(mine16(q), r_ref.at[i, z, c], loc.at[1])
            own.start()
            for k in range(1, 2 * NZ):
                r1(i, k).start()
            own.wait()

    def send_b2():
        for i in range(3):
            @pl.when((x > 0) & (y == i))
            def _():
                b1_in(i).wait_recv()
                own = pltpu.make_async_copy(s_ref.at[:, i], b_ref.at[i, :, x, i], loc.at[0])
                own.start()
                for k in FAR:
                    b2(i, k).start()
                own.wait()

    def send_b3():
        for i in range(3):
            @pl.when(y != i)
            def _():
                b2_in(i).wait_recv()

        @pl.when(c == 0)
        def _():
            for k in FAR:
                b3(k, True).start()

        @pl.when(c == 1)
        def _():
            for k in (2, 1, 3):
                b3(k, False).start()

    def send_b4():
        @pl.when(c == 0)
        def _():
            for k in range(1, NY):
                b3_in(k, True).wait_recv()
            for k in (2, 1, 3):
                b4(k).start()

        @pl.when(c == 1)
        def _():
            for k in range(1, NX):
                b3_in(k, False).wait_recv()
        hop(1)

    def get_b4():
        @pl.when(c == 0)
        def _():
            for k in range(1, NX):
                b4_in(k).wait_recv()

        @pl.when(c == 1)
        def _():
            for up in (True, False):
                ring(4, up, 4).wait_recv()

    def drain():
        for i in range(3):
            @pl.when(y == i)
            def _():
                for k in range(1, NY):
                    b2(i, k).wait_send()

        @pl.when(c == 0)
        def _():
            for k in range(1, NY):
                b3(k, True).wait_send()
            for k in range(1, NX):
                b4(k).wait_send()

        @pl.when(c == 1)
        def _():
            for k in range(1, NX):
                b3(k, False).wait_send()
            for h in range(1, 5):
                for up in (True, False):
                    ring(h, up, h - 1).wait_send()

        @pl.when(p > 0)
        def _():
            for k in range(1, NZ):
                r2(k).wait_send()
            r3().wait_send()

    def send_r2():
        for j in range(3):
            @pl.when((q != j) & (p > 0))
            def _():
                r1_in(j).wait_recv()

        @pl.when(p > 0)
        def _():
            for k in FAR:
                r2(k).start()

    def send_r3():
        @pl.when(p > 0)
        def _():
            for k in range(1, NZ):
                r2_in(k).wait_recv()
            r3().start()

    def get_r3():
        @pl.when(p > 0)
        def _():
            r3_in().wait_recv()

        @pl.when(p == 0)
        def _():
            r_ref[...] = jnp.zeros((3, NZ, 2, 2, 8, NB), F32)

    plane = tuple((k, functools.partial(on_y, f), (x == 0) & (y == 0)) for k, f in enumerate(FAR)) + tuple(
        (7 + k, functools.partial(on_x, f), x == 0) for k, f in enumerate((2, 1, 3)))

    def spread(g, arm, dev):
        return remote(part(g, z), part(g, z), ps.at[g, arm], zr.at[g], dev)

    def pick(g, k):
        return remote(part(g, z), part(g, z), gs.at[g, k - 1], gr.at[g, k - 1], on_z(k))

    def pick_in(g, k):
        o = lax.rem(z + NZ - k, NZ)
        return remote(part(g, o), part(g, o), gs.at[g, k - 1], gr.at[g, k - 1], (p, q))

    def share(g):
        lo, hi = GROUPS[g]
        return remote(t_ref.at[lo:hi], t_ref.at[lo:hi], ms.at[g], mr.at[g], mate)

    def pass_on(g):
        @pl.when(c == 1)
        def _():
            deal(g, 0).wait_recv()
            for arm, dev, cond in plane:
                @pl.when(cond)
                def _():
                    spread(g, arm, dev()).start()
            for k in FAR:
                pick(g, k).start()

    def take(g):
        @pl.when(c == 1)
        def _():
            for k in range(1, NZ):
                pick_in(g, k).wait_recv()

            @pl.when((p > 0) | (z > 0))
            def _():
                share(g).start()

        @pl.when(c == 0)
        def _():
            share(g).wait_recv()

    @pl.when(first)
    def _():
        def emit(g):
            for o in FAR + (0,):
                deal(g, o).start()

        emit(0)
        dcopy[0, 1].wait_recv()
        dcopy[1, 1].wait_recv()
        reach(0, (2, 3))
        reach(1, (2, 3))
        emit(1)
        base(2)
        reach(2, (3,))
        send_b3()
        for j in range(3):
            dcopy[j, 2].wait_recv()
        reach(0, (4, 5))
        reach(1, (4, 5))
        reach(2, (4, 5))
        emit(2)
        base(3)
        reach(3, (4, 5))
        emit(3)
        send_b4()
        base(4)
        reach(4, (5,))
        emit(4)
        base(5)
        low = lax.broadcasted_iota(jnp.int32, (TB, TB), 0) >= lax.broadcasted_iota(jnp.int32, (TB, TB), 1)
        o_ref[0, 0:TB, 0:TB] = jnp.where(low, u_ref[0].T, 0.0)
        o_ref[0, 0:TB, TB:] = jnp.zeros((TB, TB), F32)
        o_ref[0, TB:, 0:TB] = t_ref[SLOT[0, 1]].T
        o_ref[0, TB:, TB:] = jnp.where(low, u_ref[1].T, 0.0)
        o_ref[1] = jnp.zeros((NB, NB), F32)
        get_b4()
        drain()
        for g in range(NG):
            for o in range(NZ):
                deal(g, o).wait_send()

    @pl.when(late)
    def _():
        def rcols(s):
            return (s // 2, slice(None), slice(None), slice(None), slice(None), slice((s % 2) * TB, (s % 2) * TB + TB))

        def brow(s):
            return [(s // 2, j, slice((s % 2) * 2, (s % 2) * 2 + 2)) for j in range(2)]

        def apply(t):
            inv = t_ref[SLOT["L", t]]
            bt = jnp.concatenate([b_ref[k].reshape(TB, NB) for k in brow(t)], 1)
            ub = right(mm(left(inv, 1), right(bt, 0)), 0)
            lt = mmt(left(r_ref[rcols(t)].reshape(NB, TB), 1), right(inv, 1))
            r_ref[rcols(t)] = lt.reshape(NZ, 2, 2, 8, TB)
            lt = left(lt, 1)
            cur = jnp.concatenate([x_ref[0].reshape(NB, NB), x_ref[1].reshape(NB, NB)], 1) if t == 0 else acc_ref[...]
            acc_ref[...] = cur - mm(lt, ub)
            for s in range(t + 1, STEPS):
                u = t_ref[SLOT[t, s]]
                upd = mm(left(u.T, 1), ub)
                for j, k in enumerate(brow(s)):
                    b_ref[k] = b_ref[k] - upd[:, j * NB:(j + 1) * NB].reshape(2, 8, 8, NB)
                r_ref[rcols(s)] = r_ref[rcols(s)] - mm(lt, right(u, 0)).reshape(NZ, 2, 2, 8, TB)

        send_b2()
        send_r2()
        send_b3()
        pass_on(0)
        send_b4()
        pass_on(1)
        hop(2)
        pass_on(2)
        hop(3)
        take(0)
        take(1)
        hop(4)
        pass_on(3)
        take(2)
        send_r3()
        pass_on(4)
        take(3)
        pass_on(5)
        get_r3()
        get_b4()
        drain()
        take(4)
        for t in range(5):
            apply(t)
        take(5)
        apply(5)
        keep = p >= 3
        o_ref[1] = jnp.where(keep, acc_ref[:, NB:], 0.0)

        @pl.when(q >= 3)
        def _():
            o_ref[0] = jnp.where(keep, acc_ref[:, :NB], 0.0)

        row = lax.broadcasted_iota(jnp.int32, (NB, NB), 0) + p * NB
        col = lax.broadcasted_iota(jnp.int32, (NB, NB), 1)
        for j in range(3):
            @pl.when(q == j)
            def _():
                o_ref[0] = jnp.where(row >= col + j * NB, r_ref[j].reshape(NB, NB), 0.0)

        for i, j in blocks:
            @pl.when((p == i) & (q == j))
            def _():
                dcopy[i, j].wait_send()

        @pl.when(c == 1)
        def _():
            for g in range(NG):
                for k in range(1, NZ):
                    pick(g, k).wait_send()
            for arm, dev, cond in plane:
                @pl.when(cond)
                def _():
                    for g in range(NG):
                        spread(g, arm, dev()).wait_send()

            @pl.when((p > 0) | (z > 0))
            def _():
                for g in range(NG):
                    share(g).wait_send()

    for i in range(3):
        @pl.when((x == 0) & (y == i))
        def _():
            for k in range(1, NX):
                b1(i, k).wait_send()

        @pl.when((q == i) & (p > 0))
        def _():
            for k in range(1, 2 * NZ):
                r1(i, k).wait_send()


def factor(x):
    dma = pltpu.SemaphoreType.DMA
    vm = pl.BlockSpec(memory_space=VMEM)
    return pl.pallas_call(
        body,
        out_shape=jax.ShapeDtypeStruct((2, NB, NB), F32),
        in_specs=[vm],
        out_specs=vm,
        scratch_shapes=[
            VMEM((3, 2, NX, NY, 8, NB), F32), VMEM((2, NY, 8, NB), F32), VMEM((3, NZ, 2, 2, 8, NB), F32), VMEM((3, 3, NX, NY, 8, NB), F32),
            VMEM((len(TILES), TB, TB), F32), VMEM((NB, 2 * NB), F32), VMEM((2, TB, TB), F32),
            dma((3,)), dma(()), dma((7,)), dma((3,)), dma((7,)), dma((7,)), dma((8,)), dma((8,)),
            dma((15,)), dma((3,)), dma((7,)), dma((7,)), dma(()), dma(()), dma(()), dma((5,)),
            dma((NG, 8)), dma((NG,)), dma((NG, 10)), dma((NG,)), dma((NG, 7)), dma((NG, 7)), dma((NG,)), dma((NG,)),
            dma((2,)),
        ],
        compiler_params=pltpu.CompilerParams(
            collective_id=0, has_side_effects=True, vmem_limit_bytes=48 << 20),
        name="factor",
    )(x)


def shards(kernel):
    x = kernel[0].transpose(1, 0, 2).reshape(2, NX, NY, 8, NB)
    return factor(x).transpose(1, 0, 2)[None]


def solution(mesh):
    spec = P(None, "row", None, "col")
    return jax.shard_map(shards, mesh=mesh, in_specs=(spec,), out_specs=spec, check_vma=False)
```

```python
import functools

import jax
import jax.numpy as jnp
from jax import lax
from jax.experimental import pallas as pl
from jax.experimental.pallas import tpu as pltpu
from jax.sharding import PartitionSpec as P

F32 = jnp.float32
BF16 = jnp.bfloat16
NB = 256
TB = 128
STEPS = 6
NX, NY, NZ = 4, 8, 8
TILES = (("L", 0), (0, 1), ("L", 1), (0, 2), (0, 3), (1, 2), (1, 3), ("L", 2), (2, 3),
         (0, 4), (0, 5), (1, 4), (1, 5), (2, 4), (2, 5), ("L", 3), (3, 4), (3, 5),
         ("L", 4), (4, 5), ("L", 5))
SLOT = {name: k for k, name in enumerate(TILES)}
GROUPS = ((0, 2), (2, 7), (7, 15), (15, 18), (18, 20), (20, 21))
NG = len(GROUPS)
SR = TB // 8
FAR = (4, 3, 5, 2, 6, 1, 7)
VMEM = pltpu.VMEM
MESH = pl.DeviceIdType.MESH


def remote(src, dst, ssem, rsem, dev):
    return pltpu.make_async_remote_copy(
        src_ref=src, dst_ref=dst, send_sem=ssem, recv_sem=rsem,
        device_id=dev, device_id_type=MESH)


def factor_tile(M, done):
    n = len(M)
    sub = lax.broadcasted_iota(jnp.int32, (8, TB), 0)
    lane = lax.broadcasted_iota(jnp.int32, (8, TB), 1)
    M = list(M)
    E = [jnp.where(lane == sub + 8 * g, 1.0, 0.0).astype(F32) for g in range(n)]
    wide = lambda v: jnp.broadcast_to(v, (8, TB))
    for g in range(n):
        V = [{h: wide(M[h][:, 8 * g + k:8 * g + k + 1]) for h in range(g, n)} for k in range(8)]
        d = V[0][g]
        for k in range(8):
            inv = 1.0 / wide(V[k][g][k:k + 1, :])
            for j in range(k + 1, 8):
                s = wide(V[k][g][j:j + 1, :])
                V[j][g] = V[j][g] - (V[k][g] * s) * inv
                f = s * inv
                for h in range(g + 1, n):
                    V[j][h] = V[j][h] - V[k][h] * f
            if k:
                d = jnp.where(sub == k, V[k][g], d)
            mult = jnp.where(sub > k, V[k][g] * inv, 0.0)
            row_m, row_e = wide(M[g][k:k + 1, :]), wide(E[g][k:k + 1, :])
            M[g] = M[g] - mult * row_m
            E[g] = E[g] - mult * row_e
            for h in range(g + 1, n):
                c = V[k][h] * inv
                M[h] = M[h] - c * row_m
                E[h] = E[h] - c * row_e
        r = lax.rsqrt(d)
        done(g, M[g] * r, E[g] * r)


def split(a):
    hi = a.astype(BF16)
    return hi, (a - hi.astype(F32)).astype(BF16)


def left(a, axis):
    hi, lo = split(a)
    return jnp.concatenate([hi, lo, hi], axis)


def right(a, axis):
    hi, lo = split(a)
    return jnp.concatenate([hi, hi, lo], axis)


def mm(a, b):
    return jnp.dot(a, b, preferred_element_type=F32)


def mmt(a, b):
    return lax.dot_general(a, b, (((1,), (1,)), ((), ())), preferred_element_type=F32)


def body(x_ref, o_ref, b_ref, s_ref, r_ref, d_ref, t_ref, acc_ref, u_ref,
         b1s, b1r, b2s, b2r, b3s, b3r, b4s, b4r, r1s, r1r, r2s, r2r, r3s, r3r, ds, dr,
         zs, zr, ps, pr, gs, gr, ms, mr, loc):
    p = lax.axis_index("row")
    q = lax.axis_index("col")
    x = p // NY
    y = p % NY
    z = q // 2
    c = q % 2
    mate = (p, q + 1 - 2 * c)
    first = (p == 0) & (q == 0)
    late = (p > 0) | (q > 0)

    def on_x(k):
        return (lax.rem(x + k, NX) * NY + y, q)

    def on_y(k):
        return (x * NY + lax.rem(y + k, NY), q)

    def on_z(k):
        return (p, lax.rem(z + k, NZ) * 2 + c)

    barrier = pltpu.get_barrier_semaphore()

    def greet(dev):
        pl.semaphore_signal(barrier, inc=1, device_id=dev, device_id_type=MESH)

    for k in range(1, NX):
        greet(on_x(k))
    for k in range(1, NY):
        greet(on_y(k))
    for k in range(1, 2 * NZ):
        greet((p, lax.rem(q + k, 2 * NZ)))
    def part(g, o):
        lo, hi = GROUPS[g]
        return t_ref.at[lo:hi, pl.ds(pl.multiple_of(o * SR, SR), SR), :]

    def deal(g, o):
        return remote(part(g, o), part(g, o), zs.at[g, o], zr.at[g], (0, 2 * o + 1))

    def where(s, u):
        return (s // 2, u // 2, slice((s % 2) * 2, (s % 2) * 2 + 2), slice(None), slice(None),
                slice((u % 2) * TB, (u % 2) * TB + TB))

    def get(s, u):
        return d_ref[where(s, u)].reshape(TB, TB)

    def base(t):
        def done(g, u, e):
            t_ref[SLOT["L", t], 8 * g:8 * g + 8, :] = e
            if t < 2:
                u_ref[t, 8 * g:8 * g + 8, :] = u
            if t == 5 and g % 2:
                deal(NG - 1, g // 2).start()

        tile = get(t, t)
        factor_tile([tile[8 * g:8 * g + 8, :] for g in range(16)], done)

    def reach(t, cols):
        a = jnp.concatenate([get(t, u) for u in cols], 1) if len(cols) > 1 else get(t, cols[0])
        w = mm(left(t_ref[SLOT["L", t]], 1), right(a, 0))
        for k, u in enumerate(cols):
            t_ref[SLOT[t, u]] = w[:, k * TB:(k + 1) * TB]
        wr = right(w, 0)
        for s in range(t + 1, cols[-1] + 1):
            us = [u for u in cols if u >= s]
            k0 = (us[0] - cols[0]) * TB
            upd = mm(left(t_ref[SLOT[t, s]].T, 1), wr[:, k0:])
            for k, u in enumerate(us):
                d_ref[where(s, u)] = (get(s, u) - upd[:, k * TB:(k + 1) * TB]).reshape(2, 8, 8, TB)


    corner = ((1, 1), (1, 2), (2, 2))

    @pl.when(first)
    def _():
        for dev in corner:
            greet(dev)
        d_ref[0, 0] = x_ref[0]
        base(0)
        reach(0, (1,))
        base(1)
        pl.semaphore_wait(barrier, NX - 1 + NY - 1 + 2 * NZ - 1 + 3)

    near = functools.reduce(lambda a, b: a | b, [(p == i) & (q == j) for i, j in corner])
    plain = late & jnp.logical_not(near)

    @pl.when(near)
    def _():
        greet((0, 0))
        pl.semaphore_wait(barrier, NX - 1 + NY - 1 + 2 * NZ - 1 + 1)

    @pl.when(plain)
    def _():
        pl.semaphore_wait(barrier, NX - 1 + NY - 1 + 2 * NZ - 1)

    blocks = ((0, 1), (1, 1), (0, 2), (1, 2), (2, 2))
    dcopy = {}
    for k, (i, j) in enumerate(blocks):
        dcopy[i, j] = remote(x_ref.at[0], d_ref.at[i, j], ds, dr.at[k], (0, 0))

        @pl.when((p == i) & (q == j))
        def _():
            dcopy[i, j].start()

    def b1(i, k):
        o = lax.rem(x + k, NX)
        return remote(x_ref.at[:, o], s_ref, b1s.at[k - 1], b1r, on_x(k))

    def b1_in(i):
        return remote(s_ref, s_ref, b1s.at[0], b1r, (p, q))

    def b2(i, k, dealt=True):
        o = lax.rem(y + k, NY)
        src = s_ref.at[:, o] if dealt else x_ref.at[:, 0, o]
        return remote(src, b_ref.at[i, :, x, o], b2s.at[k - 1], b2r.at[i], on_y(k))

    def b2_in(i):
        return remote(b_ref.at[i, :, x, y], b_ref.at[i, :, x, y], b2s.at[0], b2r.at[i], (p, q))

    def b3(k, along_y):
        mine = b_ref.at[:, :, x, y]
        return remote(mine, mine, b3s.at[k - 1], b3r.at[k - 1], on_y(k) if along_y else on_x(k))

    def b3_in(k, along_y):
        theirs = b_ref.at[:, :, x, lax.rem(y + NY - k, NY)] if along_y else b_ref.at[:, :, lax.rem(x + NX - k, NX), y]
        return remote(theirs, theirs, b3s.at[k - 1], b3r.at[k - 1], (p, q))

    def b4(k):
        return remote(b_ref.at[:, :, x], b_ref.at[:, :, x], b4s.at[k - 1], b4r.at[k - 1], on_x(k))

    def b4_in(k):
        theirs = b_ref.at[:, :, lax.rem(x + NX - k, NX)]
        return remote(theirs, theirs, b4s.at[k - 1], b4r.at[k - 1], (p, q))

    def ring(h, up, far):
        o = lax.rem(y + (NY - far if up else far), NY)
        if h == 4:
            blk = b_ref.at[:, 0 if up else 1, :, o]
        else:
            blk = b_ref.at[:, :, :, o]
        k = 2 * (h - 1) + (0 if up else 1)
        return remote(blk, blk, b4s.at[k], b4r.at[k], on_y(1 if up else NY - 1))

    def hop(h):
        @pl.when(c == 1)
        def _():
            for up in (True, False):
                if h > 1:
                    ring(h - 1, up, h - 1).wait_recv()
            for up in (True, False):
                ring(h, up, h - 1).start()

    def mine16(o):
        return x_ref.at[0, o // 4, pl.ds(2 * lax.rem(o, 4), 2)]

    def r1(j, k):
        o = lax.rem(q + k, 2 * NZ)
        return remote(mine16(o), r_ref.at[j, o // 2, lax.rem(o, 2)], r1s.at[k - 1], r1r.at[j], (p, o))

    def r1_in(j):
        return remote(r_ref.at[j, z, c], r_ref.at[j, z, c], r1s.at[0], r1r.at[j], (p, q))

    def r2(k):
        return remote(r_ref.at[:, z, c], r_ref.at[:, z, c], r2s.at[k - 1], r2r.at[k - 1], on_z(k))

    def r2_in(k):
        o = lax.rem(z + NZ - k, NZ)
        return remote(r_ref.at[:, z, c], r_ref.at[:, o, c], r2s.at[k - 1], r2r.at[k - 1], (p, q))

    def r3():
        return remote(r_ref.at[:, :, c], r_ref.at[:, :, c], r3s, r3r, mate)

    def r3_in():
        return remote(r_ref.at[:, :, c], r_ref.at[:, :, 1 - c], r3s, r3r, mate)

    for i in range(3):
        @pl.when((x == 0) & (y == i))
        def _():
            own = pltpu.make_async_copy(x_ref.at[:, 0, i], b_ref.at[i, :, 0, i], loc.at[0])
            own.start()
            for k in (2, 1, 3):
                b1(i, k).start()
            for k in FAR:
                b2(i, k, False).start()
            own.wait()

        @pl.when((q == i) & (p > 0))
        def _():
            own = pltpu.make_async_copy(mine16(q), r_ref.at[i, z, c], loc.at[1])
            own.start()
            for k in range(1, 2 * NZ):
                r1(i, k).start()
            own.wait()

    def send_b2():
        for i in range(3):
            @pl.when((x > 0) & (y == i))
            def _():
                b1_in(i).wait_recv()
                own = pltpu.make_async_copy(s_ref.at[:, i], b_ref.at[i, :, x, i], loc.at[0])
                own.start()
                for k in FAR:
                    b2(i, k).start()
                own.wait()

    def send_b3():
        for i in range(3):
            @pl.when(y != i)
            def _():
                b2_in(i).wait_recv()

        @pl.when(c == 0)
        def _():
            for k in FAR:
                b3(k, True).start()

        @pl.when(c == 1)
        def _():
            for k in (2, 1, 3):
                b3(k, False).start()

    def send_b4():
        @pl.when(c == 0)
        def _():
            for k in range(1, NY):
                b3_in(k, True).wait_recv()
            for k in (2, 1, 3):
                b4(k).start()

        @pl.when(c == 1)
        def _():
            for k in range(1, NX):
                b3_in(k, False).wait_recv()
        hop(1)

    def get_b4():
        @pl.when(c == 0)
        def _():
            for k in range(1, NX):
                b4_in(k).wait_recv()

        @pl.when(c == 1)
        def _():
            for up in (True, False):
                ring(4, up, 4).wait_recv()

    def drain():
        for i in range(3):
            @pl.when(y == i)
            def _():
                for k in range(1, NY):
                    b2(i, k).wait_send()

        @pl.when(c == 0)
        def _():
            for k in range(1, NY):
                b3(k, True).wait_send()
            for k in range(1, NX):
                b4(k).wait_send()

        @pl.when(c == 1)
        def _():
            for k in range(1, NX):
                b3(k, False).wait_send()
            for h in range(1, 5):
                for up in (True, False):
                    ring(h, up, h - 1).wait_send()

        @pl.when(p > 0)
        def _():
            for k in range(1, NZ):
                r2(k).wait_send()
            r3().wait_send()

    def send_r2():
        for j in range(3):
            @pl.when((q != j) & (p > 0))
            def _():
                r1_in(j).wait_recv()

        @pl.when(p > 0)
        def _():
            for k in FAR:
                r2(k).start()

    def send_r3():
        @pl.when(p > 0)
        def _():
            for k in range(1, NZ):
                r2_in(k).wait_recv()
            r3().start()

    def get_r3():
        @pl.when(p > 0)
        def _():
            r3_in().wait_recv()

        @pl.when(p == 0)
        def _():
            r_ref[...] = jnp.zeros((3, NZ, 2, 2, 8, NB), F32)

    plane = tuple((k, functools.partial(on_y, f), (x == 0) & (y == 0)) for k, f in enumerate(FAR)) + tuple(
        (7 + k, functools.partial(on_x, f), x == 0) for k, f in enumerate((2, 1, 3)))

    def spread(g, arm, dev):
        return remote(part(g, z), part(g, z), ps.at[g, arm], zr.at[g], dev)

    def pick(g, k):
        return remote(part(g, z), part(g, z), gs.at[g, k - 1], gr.at[g, k - 1], on_z(k))

    def pick_in(g, k):
        o = lax.rem(z + NZ - k, NZ)
        return remote(part(g, o), part(g, o), gs.at[g, k - 1], gr.at[g, k - 1], (p, q))

    def share(g):
        lo, hi = GROUPS[g]
        return remote(t_ref.at[lo:hi], t_ref.at[lo:hi], ms.at[g], mr.at[g], mate)

    def pass_on(g):
        @pl.when(c == 1)
        def _():
            deal(g, 0).wait_recv()
            for arm, dev, cond in plane:
                @pl.when(cond)
                def _():
                    spread(g, arm, dev()).start()
            for k in FAR:
                pick(g, k).start()

    def take(g):
        @pl.when(c == 1)
        def _():
            for k in range(1, NZ):
                pick_in(g, k).wait_recv()

            @pl.when((p > 0) | (z > 0))
            def _():
                share(g).start()

        @pl.when(c == 0)
        def _():
            share(g).wait_recv()

    @pl.when(first)
    def _():
        def emit(g):
            for o in FAR + (0,):
                deal(g, o).start()

        emit(0)
        dcopy[0, 1].wait_recv()
        dcopy[1, 1].wait_recv()
        reach(0, (2, 3))
        reach(1, (2, 3))
        emit(1)
        base(2)
        reach(2, (3,))
        send_b3()
        for j in range(3):
            dcopy[j, 2].wait_recv()
        reach(0, (4, 5))
        reach(1, (4, 5))
        reach(2, (4, 5))
        emit(2)
        base(3)
        reach(3, (4, 5))
        emit(3)
        send_b4()
        base(4)
        reach(4, (5,))
        emit(4)
        base(5)
        low = lax.broadcasted_iota(jnp.int32, (TB, TB), 0) >= lax.broadcasted_iota(jnp.int32, (TB, TB), 1)
        o_ref[0, 0:TB, 0:TB] = jnp.where(low, u_ref[0].T, 0.0)
        o_ref[0, 0:TB, TB:] = jnp.zeros((TB, TB), F32)
        o_ref[0, TB:, 0:TB] = t_ref[SLOT[0, 1]].T
        o_ref[0, TB:, TB:] = jnp.where(low, u_ref[1].T, 0.0)
        o_ref[1] = jnp.zeros((NB, NB), F32)
        get_b4()
        drain()
        for g in range(NG):
            for o in range(NZ):
                deal(g, o).wait_send()

    @pl.when(late)
    def _():
        def rcols(s):
            return (s // 2, slice(None), slice(None), slice(None), slice(None), slice((s % 2) * TB, (s % 2) * TB + TB))

        def brow(s):
            return [(s // 2, j, slice((s % 2) * 2, (s % 2) * 2 + 2)) for j in range(2)]

        def apply(t):
            inv = t_ref[SLOT["L", t]]
            bt = jnp.concatenate([b_ref[k].reshape(TB, NB) for k in brow(t)], 1)
            ub = right(mm(left(inv, 1), right(bt, 0)), 0)
            lt = mmt(left(r_ref[rcols(t)].reshape(NB, TB), 1), right(inv, 1))
            r_ref[rcols(t)] = lt.reshape(NZ, 2, 2, 8, TB)
            lt = left(lt, 1)
            cur = jnp.concatenate([x_ref[0].reshape(NB, NB), x_ref[1].reshape(NB, NB)], 1) if t == 0 else acc_ref[...]
            acc_ref[...] = cur - mm(lt, ub)
            for s in range(t + 1, STEPS):
                u = t_ref[SLOT[t, s]]
                upd = mm(left(u.T, 1), ub)
                for j, k in enumerate(brow(s)):
                    b_ref[k] = b_ref[k] - upd[:, j * NB:(j + 1) * NB].reshape(2, 8, 8, NB)
                r_ref[rcols(s)] = r_ref[rcols(s)] - mm(lt, right(u, 0)).reshape(NZ, 2, 2, 8, TB)

        send_b2()
        send_r2()
        send_b3()
        pass_on(0)
        send_b4()
        pass_on(1)
        hop(2)
        pass_on(2)
        hop(3)
        take(0)
        take(1)
        hop(4)
        pass_on(3)
        take(2)
        send_r3()
        pass_on(4)
        take(3)
        pass_on(5)
        get_r3()
        get_b4()
        drain()
        for t in range(4):
            apply(t)
        take(4)
        apply(4)
        take(5)
        apply(5)
        keep = p >= 3
        o_ref[1] = jnp.where(keep, acc_ref[:, NB:], 0.0)

        @pl.when(q >= 3)
        def _():
            o_ref[0] = jnp.where(keep, acc_ref[:, :NB], 0.0)

        row = lax.broadcasted_iota(jnp.int32, (NB, NB), 0) + p * NB
        col = lax.broadcasted_iota(jnp.int32, (NB, NB), 1)
        for j in range(3):
            @pl.when(q == j)
            def _():
                o_ref[0] = jnp.where(row >= col + j * NB, r_ref[j].reshape(NB, NB), 0.0)

        for i, j in blocks:
            @pl.when((p == i) & (q == j))
            def _():
                dcopy[i, j].wait_send()

        @pl.when(c == 1)
        def _():
            for g in range(NG):
                for k in range(1, NZ):
                    pick(g, k).wait_send()
            for arm, dev, cond in plane:
                @pl.when(cond)
                def _():
                    for g in range(NG):
                        spread(g, arm, dev()).wait_send()

            @pl.when((p > 0) | (z > 0))
            def _():
                for g in range(NG):
                    share(g).wait_send()

    for i in range(3):
        @pl.when((x == 0) & (y == i))
        def _():
            for k in range(1, NX):
                b1(i, k).wait_send()

        @pl.when((q == i) & (p > 0))
        def _():
            for k in range(1, 2 * NZ):
                r1(i, k).wait_send()


def factor(x):
    dma = pltpu.SemaphoreType.DMA
    vm = pl.BlockSpec(memory_space=VMEM)
    return pl.pallas_call(
        body,
        out_shape=jax.ShapeDtypeStruct((2, NB, NB), F32),
        in_specs=[vm],
        out_specs=vm,
        scratch_shapes=[
            VMEM((3, 2, NX, NY, 8, NB), F32), VMEM((2, NY, 8, NB), F32), VMEM((3, NZ, 2, 2, 8, NB), F32), VMEM((3, 3, NX, NY, 8, NB), F32),
            VMEM((len(TILES), TB, TB), F32), VMEM((NB, 2 * NB), F32), VMEM((2, TB, TB), F32),
            dma((3,)), dma(()), dma((7,)), dma((3,)), dma((7,)), dma((7,)), dma((8,)), dma((8,)),
            dma((15,)), dma((3,)), dma((7,)), dma((7,)), dma(()), dma(()), dma(()), dma((5,)),
            dma((NG, 8)), dma((NG,)), dma((NG, 10)), dma((NG,)), dma((NG, 7)), dma((NG, 7)), dma((NG,)), dma((NG,)),
            dma((2,)),
        ],
        compiler_params=pltpu.CompilerParams(
            collective_id=0, has_side_effects=True, vmem_limit_bytes=48 << 20),
        name="factor",
    )(x)


def shards(kernel):
    x = kernel[0].transpose(1, 0, 2).reshape(2, NX, NY, 8, NB)
    return factor(x).transpose(1, 0, 2)[None]


def solution(mesh):
    spec = P(None, "row", None, "col")
    return jax.shard_map(shards, mesh=mesh, in_specs=(spec,), out_specs=spec, check_vma=False)
```
